32 devices in a mesh: groups: 2 (over y), seq: 4 (over z), dp: 4 (over x, core).
Axes of the slice: x: 2, y: 2, z: 4, core: 2. Of those that a mesh axis runs over, the one named last changes fastest.
Arguments:
- inputs: bfloat16 [8, 32768, 768], P(('groups', 'dp'), 'seq'), parts along dimension 0, may hold values from -33 to 33, as said below
- norm_gain: float32 [768], replicated, may hold values from 0.5 to 1.5
- inner_mix: bfloat16 [256, 256], replicated, may hold values from -0.375 to 0.375
- twiddle: float32 [128, 256], P('seq'), may hold values from 0.5 to 2
- outer_mix: bfloat16 [128, 128], replicated, may hold values from -0.5 to 0.5
- long_kernel: float32 [128, 256], P(None, 'seq'), may hold values from 0.5 to 2
- gate_weight: bfloat16 [768, 384], replicated, may hold values from -0.3125 to 0.3125
- out_weight: bfloat16 [768, 384], replicated, may hold values from -0.3125 to 0.3125
- cotangent: bfloat16 [8, 32768, 768], P(('groups', 'dp'), 'seq'), parts along dimension 0, may hold values from -6 to 6
Outputs:
- layer_out: bfloat16 [8, 32768, 768], P(('groups', 'dp'), 'seq'), parts along dimension 0
- input_grad: bfloat16 [8, 32768, 768], P(('groups', 'dp'), 'seq'), parts along dimension 0
- weight_grads: float32 [3072, 384], P(('groups', 'seq')), parts along dimension 0
The draws below stay inside these ranges and needn't reach their ends.
There are 2 independent parts, one for each index of `groups`. The reference program is written for one: setup_inputs(seed, part) draws one part's arguments, and reference() takes and returns one part's arrays. A program takes and returns all parts, laid end to end along the dimension named above; an argument that names none is the same for every part. Nothing has to cross between parts.
Inputs may be any that keep to these rules, and one draw needn't show every extreme that they name: `inputs`: activations' entries.
All inputs are finite; a program needn't handle non-finite values.
Results may differ from the reference program's by a relative error of at most 0.0072.
Values may be sent and summed in bfloat16 or wider, within the bound.
A program may use at most 384 MiB of HBM per device.

```python
import math
import jax
import jax.numpy as jnp
from jax import lax

OUTER = 128
INNER = 256
BLOCK = 384
CH_BLOCKS = 2
WIDTH = 768
LENGTH = 32768
BATCH = 4


def draw_inputs(key, part):
    key_vals, key_cols, key_rows = jax.random.split(key, 3)
    full_shape = (BATCH, LENGTH, WIDTH)
    col_scale = jnp.exp(jax.random.uniform(key_cols, (1, 1, WIDTH), jnp.float32, math.log(0.3), math.log(3.0)))
    values = jax.random.truncated_normal(key_vals, -4.0, 4.0, full_shape, jnp.float32)
    row_scale = jnp.exp(jax.random.uniform(key_rows, (BATCH, LENGTH, 1), jnp.float32, math.log(0.5), math.log(2.0)))
    return (values * row_scale * col_scale).astype(jnp.bfloat16)


def spiked(entries, rng, source, target, parts, factor):
    def block_of(axis_at):
        return (jnp.arange(entries.shape[axis_at]) // (entries.shape[axis_at] // parts)).reshape((-1,) + (1,) * (entries.ndim - 1 - axis_at))

    near = jax.random.permutation(rng, parts)[block_of(target)]
    other_side = (block_of(target) + parts // 2) % parts
    return jnp.where((block_of(source) == near) | (block_of(source) == other_side), factor * entries, entries)


def level_of(stream_key, dims, pieces, least, top_value):
    def one(axis_at, parts):
        steps = jax.random.uniform(jax.random.fold_in(jax.random.fold_in(stream_key, 6), axis_at), (parts,), jnp.float32, least / len(pieces), top_value / len(pieces))
        return jnp.repeat(jnp.exp(steps), dims[axis_at] // parts).reshape((-1,) + (1,) * (len(dims) - axis_at - 1))

    level = one(*pieces[0])
    for cut in pieces[1:]:
        level = level * one(*cut)
    return level


def normal_values(rng, shape, deviation, reach, cuts=(), kind=jnp.bfloat16):
    array = deviation * jax.random.normal(rng, shape, jnp.float32)
    if cuts:
        array = array * level_of(rng, shape, cuts, -0.22, 0.18)
    return jnp.clip(array, -reach, reach).astype(kind)


def noise_with(own_key, dims, scale, most, cuts, heavy, dtype=jnp.bfloat16):
    array = scale * jax.random.normal(own_key, dims, jnp.float32)
    if cuts:
        array = array * level_of(own_key, dims, cuts, -0.22, 0.18)
    return jnp.clip(spiked(array, jax.random.fold_in(own_key, 3), *heavy), -most, most).astype(dtype)


def setup_inputs(seed: int = 0, part: int = 0) -> dict:
    arg_keys = jax.random.split(jax.random.key(seed), 10)
    part_splits = jax.random.split(jax.random.fold_in(arg_keys[9], part), 10)
    return {
        "inputs": draw_inputs(jax.random.fold_in(jax.random.fold_in(arg_keys[9], part), 71), part),
        "norm_gain": jnp.clip(1.0 + 0.1 * jax.random.normal(arg_keys[1], (WIDTH,), jnp.float32), 0.5, 1.5),
        "inner_mix": normal_values(arg_keys[2], (INNER, INNER), INNER ** -0.5, 0.375),
        "twiddle": jnp.clip(jnp.exp(math.log(2.0) - 1.3862944 * jax.random.uniform(arg_keys[3], (OUTER, INNER), jnp.float32) ** level_of(arg_keys[3], (OUTER, INNER), ((0, 4),), -0.2, 0.2)), 0.5, 2.0),
        "outer_mix": normal_values(arg_keys[4], (OUTER, OUTER), OUTER ** -0.5, 0.5),
        "long_kernel": jnp.clip(jnp.exp(math.log(2.0) - 1.3862944 * jax.random.uniform(arg_keys[5], (OUTER, INNER), jnp.float32) ** level_of(arg_keys[5], (OUTER, INNER), ((1, 4),), -0.2, 0.2)), 0.5, 2.0),
        "gate_weight": normal_values(arg_keys[6], (CH_BLOCKS * BLOCK, BLOCK), BLOCK ** -0.5, 0.3125),
        "out_weight": normal_values(arg_keys[7], (CH_BLOCKS * BLOCK, BLOCK), BLOCK ** -0.5, 0.3125),
        "cotangent": noise_with(part_splits[8], (BATCH, LENGTH, WIDTH), 1.0, 6.0, ((0, 4), (1, 4)), (1, 2, 4, 2.0)),
    }


norm_eps = 1e-06

def widen(values):
    return lax.optimization_barrier(values).astype(jnp.float32)

def normalize(values, norm_gain):
    mean_square = lax.optimization_barrier(jnp.mean(values * values, axis=-1, keepdims=True))
    return values * lax.rsqrt(mean_square + norm_eps) * norm_gain

def block_apply(operand, weight):
    blocks = weight.shape[0] // weight.shape[1]
    grouped = widen(operand).reshape(operand.shape[0], blocks, weight.shape[1])
    stacked = weight.astype(jnp.float32).reshape(blocks, weight.shape[1], weight.shape[1])
    result = jnp.einsum('rki,kij->rkj', grouped, stacked)
    return result.reshape(operand.shape[0], -1)

def block_back(partner, weight):
    blocks = weight.shape[0] // weight.shape[1]
    grouped = widen(partner).reshape(partner.shape[0], blocks, weight.shape[1])
    stacked = weight.astype(jnp.float32).reshape(blocks, weight.shape[1], weight.shape[1])
    result = jnp.einsum('rkj,kij->rki', grouped, stacked)
    return result.reshape(partner.shape[0], -1)

def block_term(operand, partner):
    blocks = CH_BLOCKS
    grouped = widen(operand).reshape(operand.shape[0], blocks, BLOCK)
    other_rows = widen(partner).reshape(partner.shape[0], blocks, BLOCK)
    return jnp.einsum('rki,rkj->kij', grouped, other_rows).reshape(blocks * BLOCK, BLOCK)

def reference(inputs, norm_gain, inner_mix, twiddle, outer_mix, long_kernel, gate_weight, out_weight, cotangent):
    inner_wide = inner_mix.astype(jnp.float32)
    outer_wide = outer_mix.astype(jnp.float32)

    def one_sequence(carry, pair):
        seq_in, seq_cot = pair
        inputs_wide = seq_in.astype(jnp.float32)
        activation = normalize(inputs_wide, norm_gain).astype(jnp.bfloat16)
        grid_rows = widen(activation).reshape(OUTER, INNER, WIDTH)
        inner_out = jnp.einsum('jq,pqd->pjd', inner_wide, grid_rows)
        mixed_rows = (inner_out * twiddle[:, :, None]).astype(jnp.bfloat16)
        outer_out = jnp.einsum('ip,pjd->ijd', outer_wide, widen(mixed_rows))
        seq_mix = (outer_out * long_kernel[:, :, None]).astype(jnp.bfloat16).reshape(LENGTH, WIDTH)
        gate_pre = block_apply(activation, gate_weight)
        gate_sig = jax.nn.sigmoid(gate_pre)
        mix_wide = widen(seq_mix)
        gated_rows = (mix_wide * gate_pre * gate_sig).astype(jnp.bfloat16)
        layer_out = (inputs_wide + block_apply(gated_rows, out_weight)).astype(jnp.bfloat16)
        back_gated = block_back(seq_cot, out_weight)
        mix_grad = (back_gated * gate_pre * gate_sig).astype(jnp.bfloat16)
        gate_grad = (back_gated * mix_wide * gate_sig * (1.0 + gate_pre * (1.0 - gate_sig))).astype(jnp.bfloat16)
        act_grad = block_back(gate_grad, gate_weight)
        weight_term = jnp.concatenate([block_term(activation, gate_grad), block_term(gated_rows, seq_cot)], axis=0)
        scaled_back = (widen(mix_grad).reshape(OUTER, INNER, WIDTH) * long_kernel[:, :, None]).astype(jnp.bfloat16)
        back_outer = jnp.einsum('ip,ijd->pjd', outer_wide, widen(scaled_back)).astype(jnp.bfloat16)
        twisted = (widen(back_outer) * twiddle[:, :, None]).astype(jnp.bfloat16)
        inner_back = jnp.einsum('jq,pjd->pqd', inner_wide, widen(twisted))
        act_grad = act_grad + inner_back.reshape(LENGTH, WIDTH)
        pullback = jax.vjp(lambda wide_rows: normalize(wide_rows, norm_gain), inputs_wide)[1]
        input_grad = (seq_cot.astype(jnp.float32) + pullback(act_grad)[0]).astype(jnp.bfloat16)
        return (carry + weight_term, (layer_out, input_grad))
    start_term = jnp.zeros((2 * CH_BLOCKS * BLOCK, BLOCK), jnp.float32)
    total_term, (layer_out, input_grad) = lax.scan(one_sequence, start_term, (inputs, cotangent))
    weight_grads = total_term * (1.0 / math.sqrt(BATCH * LENGTH))
    return (layer_out, input_grad, weight_grads)
```

```python
import functools
import math

import jax
import jax.numpy as jnp
from jax import lax
from jax.experimental import pallas as pl
from jax.experimental.pallas import tpu as pltpu
from jax.sharding import PartitionSpec as P

norm_eps = 1e-06


def normalize(values, norm_gain):
    mean_square = jnp.mean(values * values, axis=-1, keepdims=True)
    return values * lax.rsqrt(mean_square + norm_eps) * norm_gain


def block_apply(operand, weight):
    blocks = weight.shape[0] // weight.shape[1]
    grouped = operand.reshape(operand.shape[0], blocks, weight.shape[1])
    stacked = weight.reshape(blocks, weight.shape[1], weight.shape[1])
    result = jnp.einsum("rki,kij->rkj", grouped, stacked, preferred_element_type=jnp.float32)
    return result.reshape(operand.shape[0], -1)


def block_back(partner, weight):
    blocks = weight.shape[0] // weight.shape[1]
    grouped = partner.reshape(partner.shape[0], blocks, weight.shape[1])
    stacked = weight.reshape(blocks, weight.shape[1], weight.shape[1])
    result = jnp.einsum("rkj,kij->rki", grouped, stacked, preferred_element_type=jnp.float32)
    return result.reshape(partner.shape[0], -1)


def block_term(operand, partner, blocks, block_size):
    grouped = operand.reshape(operand.shape[0], blocks, block_size)
    other_rows = partner.reshape(partner.shape[0], blocks, block_size)
    result = jnp.einsum("rki,rkj->kij", grouped, other_rows, preferred_element_type=jnp.float32)
    return result.reshape(blocks * block_size, block_size)


def to_columns(row_layout):
    return lax.all_to_all(row_layout, "seq", split_axis=2, concat_axis=1, tiled=True)


def to_rows(col_layout):
    return lax.all_to_all(col_layout, "seq", split_axis=1, concat_axis=2, tiled=True)


def shards_plain(
    inputs,
    norm_gain,
    inner_mix,
    twiddle,
    outer_mix,
    long_kernel,
    gate_weight,
    out_weight,
    cotangent,
):
    batch_local, rows_local, channels = inputs.shape
    inner_len = inner_mix.shape[0]
    local_outer = rows_local // inner_len
    flat_rows = batch_local * rows_local
    block_size = gate_weight.shape[1]
    blocks = gate_weight.shape[0] // block_size
    all_tokens = batch_local * lax.axis_size("dp") * rows_local * lax.axis_size("seq")
    grad_scale = 1.0 / math.sqrt(all_tokens)
    inputs_wide = inputs.reshape(flat_rows, channels).astype(jnp.float32)
    activation = normalize(inputs_wide, norm_gain).astype(jnp.bfloat16)
    grid_rows = activation.reshape(batch_local, local_outer, inner_len, channels)
    inner_out = jnp.einsum(
        "jq,bpqd->bpjd", inner_mix, grid_rows, preferred_element_type=jnp.float32
    )
    mixed_rows = (inner_out * twiddle[None, :, :, None]).astype(jnp.bfloat16)
    columns = to_columns(mixed_rows)
    outer_out = jnp.einsum("ip,bpjd->bijd", outer_mix, columns, preferred_element_type=jnp.float32)
    mixed_cols = (outer_out * long_kernel[None, :, :, None]).astype(jnp.bfloat16)
    seq_mix = to_rows(mixed_cols).reshape(flat_rows, channels)
    gate_pre = block_apply(activation, gate_weight)
    gate_sig = jax.nn.sigmoid(gate_pre)
    mix_wide = seq_mix.astype(jnp.float32)
    gated_rows = (mix_wide * gate_pre * gate_sig).astype(jnp.bfloat16)
    layer_out = (inputs_wide + block_apply(gated_rows, out_weight)).astype(jnp.bfloat16)
    cotan_rows = cotangent.reshape(flat_rows, channels)
    back_gated = block_back(cotan_rows, out_weight)
    mix_grad = (back_gated * gate_pre * gate_sig).astype(jnp.bfloat16)
    gate_grad = (back_gated * mix_wide * gate_sig * (1.0 + gate_pre * (1.0 - gate_sig))).astype(
        jnp.bfloat16
    )
    act_grad = block_back(gate_grad, gate_weight)
    weight_term = jnp.concatenate(
        [
            block_term(activation, gate_grad, blocks, block_size),
            block_term(gated_rows, cotan_rows, blocks, block_size),
        ],
        axis=0,
    )
    grad_cols = to_columns(mix_grad.reshape(batch_local, local_outer, inner_len, channels))
    scaled_back = (grad_cols.astype(jnp.float32) * long_kernel[None, :, :, None]).astype(
        jnp.bfloat16
    )
    back_outer = jnp.einsum(
        "ip,bijd->bpjd", outer_mix, scaled_back, preferred_element_type=jnp.float32
    ).astype(jnp.bfloat16)
    back_rows = to_rows(back_outer)
    twisted = (back_rows.astype(jnp.float32) * twiddle[None, :, :, None]).astype(jnp.bfloat16)
    inner_back = jnp.einsum("jq,bpjd->bpqd", inner_mix, twisted, preferred_element_type=jnp.float32)
    act_grad = act_grad + inner_back.reshape(flat_rows, channels)
    pullback = jax.vjp(lambda wide_rows: normalize(wide_rows, norm_gain), inputs_wide)[1]
    input_grad = (cotan_rows.astype(jnp.float32) + pullback(act_grad)[0]).astype(jnp.bfloat16)
    shard_term = lax.psum_scatter(weight_term, "seq", scatter_dimension=0, tiled=True)
    weight_grads = lax.psum(shard_term, "dp") * grad_scale
    return (layer_out.reshape(inputs.shape), input_grad.reshape(inputs.shape), weight_grads)


def dot(lhs, rhs, lhs_dim=1, rhs_dim=0):
    return lax.dot_general(
        lhs, rhs, (((lhs_dim,), (rhs_dim,)), ((), ())), preferred_element_type=jnp.float32
    )


def row_scale(wide, channels):
    return lax.rsqrt(jnp.sum(wide * wide, axis=-1, keepdims=True) / channels + norm_eps)


def pick_column(table):
    lanes = lax.broadcasted_iota(jnp.int32, table.shape, 1)
    return jnp.sum(jnp.where(lanes == pl.program_id(0), table, 0.0), axis=-1, keepdims=True)


def gate_terms(act, weight):
    gate_pre = dot(act, weight)
    gate_sig = jax.nn.sigmoid(gate_pre)
    return gate_pre, gate_sig


def enter_kernel(x_ref, gain_ref, inner_ref, twiddle_ref, act_ref, mixed_ref):
    wide = x_ref[...].astype(jnp.float32)
    act = (wide * row_scale(wide, wide.shape[1]) * gain_ref[...]).astype(jnp.bfloat16)
    act_ref[...] = act
    mixed = dot(inner_ref[...], act[:, : mixed_ref.shape[-1]]) * pick_column(twiddle_ref[...])
    mixed_ref[...] = mixed.astype(jnp.bfloat16).reshape(mixed_ref.shape)


def inner_kernel(act_ref, inner_ref, twiddle_ref, mixed_ref):
    mixed = dot(inner_ref[...], act_ref[...]) * pick_column(twiddle_ref[...])
    mixed_ref[...] = mixed.astype(jnp.bfloat16).reshape(mixed_ref.shape)


def mix_grad_kernel(act_ref, cot_ref, gate_ref, out_ref, *grad_refs):
    for k, ref in enumerate(grad_refs):
        size = ref.shape[-1]
        part = slice(k * size, (k + 1) * size)
        gate_pre, gate_sig = gate_terms(act_ref[:, part], gate_ref[part, :])
        back = dot(cot_ref[:, part], out_ref[part, :], 1, 1)
        ref[...] = (back * gate_pre * gate_sig).astype(jnp.bfloat16).reshape(ref.shape)


def gate_kernel(blocks, x_ref, act_ref, cot_ref, gate_ref, out_ref, *refs):
    seq_refs = refs[:blocks]
    layer_ref, grad_ref, term_ref = refs[blocks:]
    size = gate_ref.shape[1]

    @pl.when(pl.program_id(0) == 0)
    def _():
        term_ref[...] = jnp.zeros_like(term_ref)

    for k, seq_ref in enumerate(seq_refs):
        part = slice(k * size, (k + 1) * size)
        act = act_ref[:, part]
        cot = cot_ref[:, part]
        gate_pre, gate_sig = gate_terms(act, gate_ref[part, :])
        mix = seq_ref[...].reshape(act.shape).astype(jnp.float32)
        gated = (mix * gate_pre * gate_sig).astype(jnp.bfloat16)
        layer_ref[:, part] = (
            x_ref[:, part].astype(jnp.float32) + dot(gated, out_ref[part, :])
        ).astype(jnp.bfloat16)
        back = dot(cot, out_ref[part, :], 1, 1)
        grad = (back * mix * gate_sig * (1.0 + gate_pre * (1.0 - gate_sig))).astype(jnp.bfloat16)
        grad_ref[:, part] = grad
        term_ref[part, :] += dot(act, grad, 0, 0)
        low = (blocks + k) * size
        term_ref[low : low + size, :] += dot(gated, cot, 0, 0)


def leave_kernel(
    blocks, x_ref, cot_ref, grad_ref, gain_ref, inner_t_ref, twiddle_ref, gate_t_ref, *refs
):
    back_refs = refs[:blocks]
    result_ref = refs[blocks]
    size = gate_t_ref.shape[1]
    column = pick_column(twiddle_ref[...])
    parts = []
    for k, back_ref in enumerate(back_refs):
        part = slice(k * size, (k + 1) * size)
        rows = back_ref[...].reshape(x_ref.shape[0], size).astype(jnp.float32)
        twisted = (rows * column).astype(jnp.bfloat16)
        parts.append(
            dot(grad_ref[:, part], gate_t_ref[part, :]) + dot(inner_t_ref[...], twisted)
        )
    act_grad = jnp.concatenate(parts, axis=1)
    wide = x_ref[...].astype(jnp.float32)
    scale = row_scale(wide, wide.shape[1])
    pulled = act_grad * gain_ref[...]
    share = jnp.sum(pulled * wide, axis=-1, keepdims=True) / wide.shape[1]
    grad = pulled * scale - wide * (scale * scale * scale * share)
    result_ref[...] = (cot_ref[...].astype(jnp.float32) + grad).astype(jnp.bfloat16)


def shards_fast(
    inputs,
    norm_gain,
    inner_mix,
    twiddle,
    outer_mix,
    long_kernel,
    gate_weight,
    out_weight,
    cotangent,
):
    batch, rows_local, channels = inputs.shape
    inner_len = inner_mix.shape[0]
    outer_len = outer_mix.shape[0]
    local_outer = rows_local // inner_len
    flat = batch * rows_local
    steps = batch * local_outer
    size = gate_weight.shape[1]
    blocks = gate_weight.shape[0] // size
    seq_n = lax.axis_size("seq")
    dp_n = lax.axis_size("dp")
    cols = inner_len // seq_n
    grad_scale = 1.0 / math.sqrt(batch * dp_n * rows_local * seq_n)
    bf16 = jnp.bfloat16

    x = inputs.reshape(flat, channels)
    cot = cotangent.reshape(flat, channels)
    gain = norm_gain.reshape(1, channels)
    twiddle_cols = jnp.tile(twiddle.T, (1, batch))
    inner_t = inner_mix.T
    gate_t = gate_weight.reshape(blocks, size, size).swapaxes(1, 2).reshape(blocks * size, size)

    row_spec = pl.BlockSpec((inner_len, channels), lambda r: (r, 0))
    swap_spec = pl.BlockSpec((seq_n, 1, cols, size), lambda r: (0, r, 0, 0))
    row_shape = jax.ShapeDtypeStruct((flat, channels), bf16)
    swap_shape = jax.ShapeDtypeStruct((seq_n, steps, cols, size), bf16)

    def whole(array):
        return pl.BlockSpec(array.shape, lambda r: (0,) * array.ndim)

    def cost(matmuls, arrays):
        return pl.CostEstimate(
            flops=2 * flat * channels * matmuls,
            bytes_accessed=int(2 * flat * channels * arrays),
            transcendentals=0,
        )

    def exchange(held):
        return lax.all_to_all(held, "seq", split_axis=0, concat_axis=0, tiled=True)

    act, first = pl.pallas_call(
        enter_kernel,
        grid=(steps,),
        in_specs=[row_spec, whole(gain), whole(inner_mix), whole(twiddle_cols)],
        out_specs=[row_spec, swap_spec],
        out_shape=[row_shape, swap_shape],
        cost_estimate=cost(inner_len // blocks, 2.5),
        name="enter",
    )(x, gain, inner_mix, twiddle_cols)
    columns = [exchange(first)]
    for k in range(1, blocks):
        mixed = pl.pallas_call(
            inner_kernel,
            grid=(steps,),
            in_specs=[
                pl.BlockSpec((inner_len, size), functools.partial(lambda k, r: (r, k), k)),
                whole(inner_mix),
                whole(twiddle_cols),
            ],
            out_specs=swap_spec,
            out_shape=swap_shape,
            cost_estimate=cost(inner_len // blocks, 1),
            name="inner",
        )(act, inner_mix, twiddle_cols)
        columns.append(exchange(mixed))

    mix_grad = pl.pallas_call(
        mix_grad_kernel,
        grid=(steps,),
        in_specs=[row_spec, row_spec, whole(gate_weight), whole(out_weight)],
        out_specs=[swap_spec] * blocks,
        out_shape=[swap_shape] * blocks,
        cost_estimate=cost(2 * size, 3),
        name="mix_grad",
    )(act, cot, gate_weight, out_weight)
    grad_cols = [exchange(part) for part in mix_grad]

    by_column = (seq_n, batch, local_outer, cols, size)

    def gather_outer(part):
        return part.reshape(by_column).swapaxes(0, 1).reshape(batch, outer_len, cols, size)

    def split_outer(part):
        part = part.reshape(batch, seq_n, local_outer, cols, size).swapaxes(0, 1)
        return part.reshape(seq_n, steps, cols, size)

    def outer_forward(part):
        out = jnp.einsum(
            "ip,bpjd->bijd", outer_mix, gather_outer(part), preferred_element_type=jnp.float32
        )
        return split_outer((out * long_kernel[None, :, :, None]).astype(bf16))

    def outer_backward(part):
        wide = gather_outer(part).astype(jnp.float32)
        scaled = (wide * long_kernel[None, :, :, None]).astype(bf16)
        out = jnp.einsum("ip,bijd->bpjd", outer_mix, scaled, preferred_element_type=jnp.float32)
        return split_outer(out.astype(bf16))

    seq_mix = [exchange(outer_forward(part)) for part in columns]
    back_rows = [exchange(outer_backward(part)) for part in grad_cols]

    term_rows = 2 * blocks * size
    layer_out, gate_grad, term = pl.pallas_call(
        functools.partial(gate_kernel, blocks),
        grid=(steps,),
        in_specs=[row_spec] * 3 + [whole(gate_weight), whole(out_weight)] + [swap_spec] * blocks,
        out_specs=[row_spec, row_spec, pl.BlockSpec((term_rows, size), lambda r: (0, 0))],
        out_shape=[row_shape, row_shape, jax.ShapeDtypeStruct((term_rows, size), jnp.float32)],
        cost_estimate=cost(5 * size, 6),
        name="gate",
    )(x, act, cot, gate_weight, out_weight, *seq_mix)

    piece = term_rows // seq_n // dp_n
    term = term.reshape(seq_n, dp_n, piece, size).swapaxes(0, 1)
    term = term.reshape(dp_n * seq_n * piece, size)
    term = lax.psum_scatter(term, "dp", scatter_dimension=0, tiled=True)
    term = lax.psum_scatter(term, "seq", scatter_dimension=0, tiled=True)
    weight_grads = lax.all_gather(term * grad_scale, "dp", axis=0, tiled=True)

    input_grad = pl.pallas_call(
        functools.partial(leave_kernel, blocks),
        grid=(steps,),
        in_specs=[row_spec] * 3
        + [whole(gain), whole(inner_t), whole(twiddle_cols), whole(gate_t)]
        + [swap_spec] * blocks,
        out_specs=row_spec,
        out_shape=row_shape,
        cost_estimate=cost(size + inner_len, 5),
        name="leave",
    )(x, cot, gate_grad, gain, inner_t, twiddle_cols, gate_t, *back_rows)
    return (layer_out.reshape(inputs.shape), input_grad.reshape(inputs.shape), weight_grads)


def shards(*arrays):
    cols = arrays[5].shape[1]
    pieces = 2 * arrays[6].shape[0] // lax.axis_size("seq") // lax.axis_size("dp")
    if cols % 16 == 0 and pieces % 8 == 0:
        return shards_fast(*arrays)
    return shards_plain(*arrays)


def solution(mesh):
    return jax.shard_map(
        shards,
        mesh=mesh,
        in_specs=(
            P(("groups", "dp"), "seq", None),
            P(),
            P(),
            P("seq", None),
            P(),
            P(None, "seq"),
            P(),
            P(),
            P(("groups", "dp"), "seq", None),
        ),
        out_specs=(
            P(("groups", "dp"), "seq", None),
            P(("groups", "dp"), "seq", None),
            P(("groups", "seq"), None),
        ),
        check_vma=False,
    )
```
